32 devices in a mesh: gx: 8 (over y, x, core), gy: 4 (over z).
Axes of the slice: x: 2, y: 2, z: 4, core: 2. Of those that a mesh axis runs over, the one named last changes fastest.
Arguments:
- displacement: float32 [3, 24, 32, 128], P(None, 'gx', 'gy'), may hold values from -0.1 to 0.1
- velocity: float32 [3, 24, 32, 128], P(None, 'gx', 'gy'), may hold values from -0.6 to 0.6
- bone: int32 [24, 32, 128], P('gx', 'gy'), may hold values 0 or 1
- broken: int32 [4, 24, 32, 128], P(None, 'gx', 'gy'), may hold values from 0 to 65535, as said below
Outputs:
- velocity_end: float32 [3, 24, 32, 128], P(None, 'gx', 'gy')
- damage: float32 [24, 32, 128], P('gx', 'gy')
The draws below stay inside these ranges and needn't reach their ends.
Inputs may be any that keep to these rules, and one draw needn't show every extreme that they name: 1 marks bone, 0 void. `broken`: only the bits that flag bonds are used: bits 0 to 15 of word 0 and bits 0 to 14 of words 1 to 3.
All inputs are finite; a program needn't handle non-finite values. No bound on the sum of `bone` on one device may be relied on, other than what follows from the above.
Results may differ from the reference program's by a relative error of at most 0.000069.
Values sent between devices are 32-bit elements; how exact they have to be, the bound alone decides.
A program may use at most 128 MiB of HBM per device.

```python
import jax
import jax.numpy as jnp
from jax import lax

NZ = 128
STEPS = 2
NX = 24
NY = 32


def draw_broken(key, part):
    subkeys = jax.random.split(jax.random.fold_in(key, 17), 12)
    packed = []
    for position in range(4):
        ceiling = 65536 if position == 0 else 32768
        merged = jax.random.randint(subkeys[3 * position], (NX, NY, NZ), 0, ceiling, dtype=jnp.int32)
        for repeat in range(1, 3):
            another = jax.random.randint(subkeys[3 * position + repeat], (NX, NY, NZ), 0, ceiling, dtype=jnp.int32)
            merged = jnp.bitwise_and(merged, another)
        packed.append(merged)
    return jnp.stack(packed)


def plant(result, key, least, high):
    place = [jax.random.randint(jax.random.fold_in(key, axis), (), 0, length) for axis, length in enumerate(result.shape)]
    longest = result.shape.index(max(result.shape))
    next_to = place[:longest] + [(place[longest] + 1) % result.shape[longest]] + place[longest + 1:]
    return result.at[tuple(place)].set(least).at[tuple(next_to)].set(high)


def block_scale(rng, shape, cuts, low, high):
    def one(dim, shards_of):
        heights = jax.random.uniform(jax.random.fold_in(jax.random.fold_in(rng, 6), dim), (shards_of,), jnp.float32, low / len(cuts), high / len(cuts))
        return jnp.repeat(jnp.exp(heights), shape[dim] // shards_of).reshape((-1,) + (1,) * (len(shape) - dim - 1))

    loudness = one(*cuts[0])
    for cut in cuts[1:]:
        loudness = loudness * one(*cut)
    return loudness


def scatter_about(key, extent, scale, reach, shards=(), kind=jnp.bfloat16):
    values = scale * jax.random.normal(key, extent, jnp.float32)
    if shards:
        values = values * block_scale(key, extent, shards, -0.22, 0.18)
    return jnp.clip(values, -reach, reach).astype(kind)


def setup_inputs(seed: int = 0) -> dict:
    keys = jax.random.split(jax.random.key(seed), 5)
    displacement = scatter_about(keys[0], (3, NX, NY, NZ), 0.025, 0.1, ((1, 8), (2, 4)), jnp.float32)
    velocity = scatter_about(keys[1], (3, NX, NY, NZ), 0.2, 0.6, ((1, 8), (2, 4)), jnp.float32)
    bone = plant((jax.random.randint(keys[2], (NX, NY, NZ), 0, 8) < 7).astype(jnp.int32), jax.random.fold_in(keys[2], 1), 0, 1)
    broken = draw_broken(jax.random.fold_in(keys[4], 71), 0)
    return {"displacement": displacement, "velocity": velocity, "bone": bone, "broken": broken}


BULK_TERM = -50.0
SHEAR_TERM = 1500.0
TIME_STEP = 0.1
STRETCH_CRITICAL = 0.04
STRETCH_WIDTH = 0.01
DIRECTION_EPS = 1e-06

def half_bonds():
    listed = []
    for step_x in range(0, 4):
        for step_y in range(-3, 4):
            for step_z in range(-3, 4):
                forward_half = step_x > 0 or (step_x == 0 and (step_y > 0 or (step_y == 0 and step_z > 0)))
                if forward_half and step_x * step_x + step_y * step_y + step_z * step_z <= 9:
                    listed.append((step_x, step_y, step_z))
    return listed

def flag_place(number):
    if number < 16:
        return (0, number)
    return (1 + (number - 16) // 15, (number - 16) % 15)

def reference(displacement, velocity, bone, broken):
    forward_bonds = half_bonds()
    table_rows = []
    for number, (step_x, step_y, step_z) in enumerate(forward_bonds):
        word_index, bit_index = flag_place(number)
        table_rows.append([step_x, step_y, step_z, word_index, bit_index])
    bond_table = jnp.array(table_rows, dtype=jnp.int32)
    size_x, size_y, size_z = bone.shape
    bone_field = bone.astype(jnp.float32)
    bone_padded = jnp.pad(bone_field, 3)[None]
    pad_three = ((0, 0), (3, 3), (3, 3), (3, 3))

    def corner(entry):
        return (jnp.int32(0), entry[0] + 3, entry[1] + 3, entry[2] + 3)

    def neighbour(padded, entry):
        return lax.dynamic_slice(padded, corner(entry), (padded.shape[0], size_x, size_y, size_z))

    def add_remote(remote_part, contrib, entry):
        window = lax.dynamic_slice(remote_part, corner(entry), contrib.shape)
        return lax.dynamic_update_slice(remote_part, window + contrib, corner(entry))

    def geometry(moved_padded, moved_field, entry):
        nearby = neighbour(moved_padded, entry)
        offset = entry[:3].astype(jnp.float32)
        rel_x = nearby[0] - moved_field[0] + offset[0]
        rel_y = nearby[1] - moved_field[1] + offset[1]
        rel_z = nearby[2] - moved_field[2] + offset[2]
        squared = rel_x * rel_x + rel_y * rel_y + rel_z * rel_z
        length = jnp.sqrt(squared)
        natural = jnp.sqrt(offset[0] * offset[0] + offset[1] * offset[1] + offset[2] * offset[2])
        extension = length - natural
        stretch = extension / natural
        flagged = jnp.bitwise_and(jnp.right_shift(broken[entry[3]], entry[4]), 1).astype(jnp.float32)
        intact = bone_field * neighbour(bone_padded, entry)[0] * (1.0 - flagged)
        weight = intact * jax.nn.sigmoid((STRETCH_CRITICAL - stretch) / STRETCH_WIDTH)
        spread = jnp.sqrt(squared + DIRECTION_EPS)
        unit = jnp.stack([rel_x / spread, rel_y / spread, rel_z / spread])
        return (intact, weight, stretch, extension, natural, unit)

    def bond_sums(moved_field):
        moved_padded = jnp.pad(moved_field, pad_three)

        def visit_bond(running, entry):
            local_part, remote_part = running
            intact, weight, stretch, extension, natural, unit = geometry(moved_padded, moved_field, entry)
            contrib = jnp.stack([weight * extension, intact * natural, weight * natural])
            return ((local_part + contrib, add_remote(remote_part, contrib, entry)), None)
        initial = (jnp.zeros((3, size_x, size_y, size_z), jnp.float32), jnp.zeros((3, size_x + 6, size_y + 6, size_z + 6), jnp.float32))
        (local_part, remote_part), ignored = lax.scan(visit_bond, initial, bond_table)
        return local_part + remote_part[:, 3:-3, 3:-3, 3:-3]

    def bond_forces(moved_field, scaled, inverse):
        moved_padded = jnp.pad(moved_field, pad_three)
        ratio_padded = jnp.pad(jnp.stack([scaled, inverse]), pad_three)

        def visit_bond(running, entry):
            local_part, remote_part = running
            intact, weight, stretch, extension, natural, unit = geometry(moved_padded, moved_field, entry)
            nearby = neighbour(ratio_padded, entry)
            magnitude = weight * (BULK_TERM * (scaled + nearby[0]) + SHEAR_TERM * stretch * (inverse + nearby[1]))
            contrib = magnitude[None] * unit
            return ((local_part + contrib, add_remote(remote_part, -contrib, entry)), None)
        initial = (jnp.zeros((3, size_x, size_y, size_z), jnp.float32), jnp.zeros((3, size_x + 6, size_y + 6, size_z + 6), jnp.float32))
        (local_part, remote_part), ignored = lax.scan(visit_bond, initial, bond_table)
        return local_part + remote_part[:, 3:-3, 3:-3, 3:-3]
    current = displacement
    current_speed = velocity
    for step_index in range(STEPS):
        totals = bond_sums(current)
        if step_index == 0:
            volume = jnp.maximum(totals[1], 1.0)
            inverse = 1.0 / volume
        dilatation = 3.0 * totals[0] / volume
        scaled = dilatation * inverse
        force_field = bond_forces(current, scaled, inverse)
        current_speed = current_speed + TIME_STEP * force_field
        if step_index < STEPS - 1:
            current = current + TIME_STEP * current_speed
    damage = 1.0 - totals[2] / volume
    return (current_speed, damage)
```

```python
import functools
import math

import jax
import jax.numpy as jnp
from jax import lax
from jax.experimental import pallas as pl
from jax.experimental.pallas import tpu as pltpu
from jax.sharding import PartitionSpec as P

STEPS = 2
REACH = 3

BULK_TERM = -50.0
SHEAR_TERM = 1500.0
TIME_STEP = 0.1
STRETCH_CRITICAL = 0.04
STRETCH_WIDTH = 0.01
DIRECTION_EPS = 1e-06
LOG2_E = math.log2(math.e)

ROW = 4

AROUND = [(dx, dy) for dx in (-1, 0, 1) for dy in (-1, 0, 1) if (dx, dy) != (0, 0)]


def half_bonds():
    listed = []
    for step_x in range(0, 4):
        for step_y in range(-3, 4):
            for step_z in range(-3, 4):
                forward_half = step_x > 0 or (
                    step_x == 0 and (step_y > 0 or (step_y == 0 and step_z > 0))
                )
                if forward_half and step_x * step_x + step_y * step_y + step_z * step_z <= 9:
                    listed.append((step_x, step_y, step_z))
    return listed


def flag_place(number):
    if number < 16:
        return (0, number)
    return (1 + (number - 16) // 15, (number - 16) % 15)


def every_bond():
    listed = []
    for number, (step_x, step_y, step_z) in enumerate(half_bonds()):
        listed.append((step_x, step_y, step_z, number, False))
        listed.append((-step_x, -step_y, -step_z, number, True))
    return listed


def packed_rows(fields, layers):
    return -(-fields * layers * REACH // 8) * 8


class Exchange:
    def __init__(self, own, packed, from_x, from_y, send_sem, recv_sem, base, sides, place, has):
        self.own, self.packed = own, packed
        self.from_x, self.from_y = from_x, from_y
        self.send_sem, self.recv_sem, self.base = send_sem, recv_sem, base
        self.sides, self.place, self.has = sides, place, has
        self.low_dx = min(-dx for dx, dy in sides)

    def copy(self, number):
        dx, dy = self.sides[number]
        if dy == 0:
            source = self.own
            target = self.from_x.at[0 if dx == 1 else 1]
        else:
            source = self.packed.at[0 if dy == -1 else 1]
            target = self.from_y.at[-dx - self.low_dx, 0 if dy == 1 else 1]
        return pltpu.make_async_remote_copy(
            src_ref=source,
            dst_ref=target,
            send_sem=self.send_sem.at[self.base + number],
            recv_sem=self.recv_sem.at[self.base + number],
            device_id={"gx": self.place[0] + dx, "gy": self.place[1] + dy},
            device_id_type=pl.DeviceIdType.MESH,
        )

    def pack(self):
        fields, layers, rows = self.own.shape[:3]
        for field in range(fields):
            for layer in range(layers):
                at = (field * layers + layer) * REACH
                self.packed[0, at : at + REACH] = self.own[field, layer, 0:REACH]
                self.packed[1, at : at + REACH] = self.own[field, layer, rows - REACH : rows]

    def clear(self):
        for dx, dy in self.sides:
            if dy == 0:
                slot = self.from_x.at[0 if dx == 1 else 1]
            else:
                slot = self.from_y.at[-dx - self.low_dx, 0 if dy == 1 else 1]

            @pl.when(jnp.logical_not(self.has(-dx, -dy)))
            def _():
                slot[...] = jnp.zeros(slot.shape, slot.dtype)

    def start(self):
        for number, (dx, dy) in enumerate(self.sides):

            @pl.when(self.has(dx, dy))
            def _():
                self.copy(number).start()

    def wait_recv(self):
        for number, (dx, dy) in enumerate(self.sides):

            @pl.when(self.has(-dx, -dy))
            def _():
                self.copy(number).wait_recv()

    def wait_send(self):
        for number, (dx, dy) in enumerate(self.sides):

            @pl.when(self.has(dx, dy))
            def _():
                self.copy(number).wait_send()

    def assemble(self, extended, dxs):
        fields, layers, rows = self.own.shape[:3]
        for dx in dxs:
            for field in range(fields):
                for layer in range(layers):
                    whole = (dx + 1) * layers + layer
                    at = (field * layers + layer) * REACH
                    if dx == 0:
                        tile = self.own[field, layer]
                    else:
                        tile = self.from_x[0 if dx == -1 else 1, field, layer]
                    y_at = dx - self.low_dx
                    extended[field, whole, ROW : ROW + rows] = tile
                    extended[field, whole, ROW - REACH : ROW] = self.from_y[y_at, 0, at : at + REACH]
                    extended[field, whole, ROW + rows : ROW + rows + REACH] = self.from_y[
                        y_at, 1, at : at + REACH
                    ]


def spread_rolls(rolled, fields, change=None):
    layers, rows, depth = rolled.shape[2:]

    @pl.loop(0, layers)
    def _(layer):
        for field in fields:
            for half in range(0, rows, 8):
                tile = rolled[REACH, field, layer, half : half + 8]
                for step_z in range(-REACH, REACH + 1):
                    if step_z == 0:
                        continue
                    moved = pltpu.roll(tile, (-step_z) % depth, 1)
                    if change is not None:
                        moved = change(moved, field, step_z)
                    rolled[REACH + step_z, field, layer, half : half + 8] = moved


def kernel(
    count_x, count_y,
    u_ref, v_ref, bone_ref, words_ref,
    velocity_ref, damage_ref,
    own1, pack1, fx1, fy1,
    packw, fxw, fyw,
    own2, pack2, fx2, fy2,
    own3, pack3, fx3, fy3,
    own4, pack4, fx4, fy4,
    near, near_words, ratio, masks, pulls, stretches, volumes,
    send_sem, recv_sem,
):
    place = (lax.axis_index("gx"), lax.axis_index("gy"))
    layers, rows, depth = bone_ref.shape
    bonds = every_bond()

    def has(dx, dy):
        there = None
        for at, step, count in ((place[0], dx, count_x), (place[1], dy, count_y)):
            if step == 0:
                continue
            good = at > 0 if step < 0 else at < count - 1
            there = good if there is None else jnp.logical_and(there, good)
        return there

    def exchange(own, packed, from_x, from_y, base, sides):
        return Exchange(own, packed, from_x, from_y, send_sem, recv_sem, base, sides, place, has)

    word_sides = [(dx, dy) for dx, dy in AROUND if dx >= 0]
    count = len(AROUND)
    first = exchange(own1, pack1, fx1, fy1, 0, AROUND)
    flags = exchange(words_ref, packw, fxw, fyw, count, word_sides)
    base = count + len(word_sides)
    second = exchange(own2, pack2, fx2, fy2, base, AROUND)
    third = exchange(own3, pack3, fx3, fy3, base + count, AROUND)
    fourth = exchange(own4, pack4, fx4, fy4, base + 2 * count, AROUND)
    exchanges = (first, flags, second, third, fourth)

    barrier = pltpu.get_barrier_semaphore()
    expected = jnp.int32(0)
    for dx, dy in AROUND:
        there = has(dx, dy)
        expected = expected + there.astype(jnp.int32)

        @pl.when(there)
        def _():
            pl.semaphore_signal(
                barrier,
                inc=1,
                device_id={"gx": place[0] + dx, "gy": place[1] + dy},
                device_id_type=pl.DeviceIdType.MESH,
            )

    for part in exchanges:
        part.packed[...] = jnp.zeros(part.packed.shape, part.packed.dtype)
        part.clear()
    for axis in range(3):
        own1[axis] = u_ref[axis]
    own1[3] = bone_ref[...].astype(jnp.float32)
    first.pack()
    flags.pack()
    pl.semaphore_wait(barrier, expected)
    first.start()
    flags.start()

    lane = lax.broadcasted_iota(jnp.int32, (8, depth), 1)

    def shifted(moved, field, step_z):
        if field == 2:
            return moved + float(step_z)
        if field == 3:
            inside = (lane + step_z >= 0) & (lane + step_z < depth)
            return jnp.where(inside, moved, 0.0)
        return moved

    for step_index in range(STEPS):
        opening = step_index == 0
        last_step = step_index == STEPS - 1
        source = first if opening else third
        source.wait_recv()
        source.assemble(near.at[REACH], (-1, 0, 1))
        spread_rolls(near, range(4 if opening else 3), shifted)
        if opening:
            flags.wait_recv()
            flags.assemble(near_words.at[REACH], (-1, 0))
            spread_rolls(near_words, range(4))
        moving = u_ref if opening else own3
        ratios = second if opening else fourth

        @pl.loop(0, layers)
        def _(layer):
            here = [moving[axis, layer] for axis in range(3)]
            total = jnp.zeros((rows, depth), jnp.float32)
            sums = {}
            if opening:
                words_here = [words_ref[word, layer] for word in range(4)]
            for number, (step_x, step_y, step_z, flag, backward) in enumerate(bonds):
                low = ROW + step_y
                rel = []
                for axis, step in enumerate((step_x, step_y, 0)):
                    far = near[REACH + step_z, axis, layer + layers + step_x, low : low + rows]
                    rel.append(far - (here[axis] - float(step)))
                squared = rel[0] * rel[0] + rel[1] * rel[1] + rel[2] * rel[2]
                length = squared * lax.rsqrt(jnp.maximum(squared, 1e-30))
                norm = step_x * step_x + step_y * step_y + step_z * step_z
                natural = math.sqrt(norm)
                extension = length - natural
                power = extension * (LOG2_E / (STRETCH_WIDTH * natural)) - (
                    STRETCH_CRITICAL * LOG2_E / STRETCH_WIDTH
                )
                if opening:
                    word, bit = flag_place(flag)
                    if backward:
                        held = near_words[
                            REACH + step_z, word, layer + layers + step_x, low : low + rows
                        ]
                    else:
                        held = words_here[word]
                    far_bone = near[REACH + step_z, 3, layer + layers + step_x, low : low + rows]
                    intact = jnp.where((held & (1 << bit)) == 0, far_bone, 0.0)
                    masks[number, layer] = intact
                    sums[norm] = sums[norm] + intact if norm in sums else intact
                else:
                    intact = masks[number, layer]
                weight = intact / (1.0 + jnp.exp2(power))
                if last_step:
                    sums[norm] = sums[norm] + weight if norm in sums else weight
                total = total + weight * extension
                stretches[number, layer] = extension * (1.0 / natural)
                pull = weight * lax.rsqrt(squared + DIRECTION_EPS)
                for axis in range(3):
                    pulls[number, axis, layer] = pull * rel[axis]
            bone_here = own1[3, layer]
            weighted = jnp.zeros((rows, depth), jnp.float32)
            for norm, value in sums.items():
                weighted = weighted + value * math.sqrt(norm)
            weighted = weighted * bone_here
            if opening:
                volume = jnp.maximum(weighted, 1.0)
                inverse = 1.0 / volume
                volumes[layer] = inverse
                own2[1, layer] = inverse * SHEAR_TERM
            else:
                inverse = volumes[layer]
            if last_step:
                damage_ref[layer] = 1.0 - weighted * inverse
            scaled = (3.0 * (total * bone_here) * inverse) * inverse
            ratios.own[0, layer] = scaled * BULK_TERM

        ratios.pack()
        ratios.start()
        ratios.wait_recv()
        ratios.assemble(ratio.at[REACH], (-1, 0, 1))
        spread_rolls(ratio, range(2 if opening else 1))

        @pl.loop(0, layers)
        def _(layer):
            scaled = ratios.own[0, layer]
            inverse = own2[1, layer]
            force = [jnp.zeros((rows, depth), jnp.float32) for axis in range(3)]
            for number, (step_x, step_y, step_z, flag, backward) in enumerate(bonds):
                low = ROW + step_y
                far = [
                    ratio[REACH + step_z, kind, layer + layers + step_x, low : low + rows]
                    for kind in range(2)
                ]
                magnitude = (scaled + far[0]) + stretches[number, layer] * (inverse + far[1])
                for axis in range(3):
                    force[axis] = force[axis] + magnitude * pulls[number, axis, layer]
            bone_here = own1[3, layer] * TIME_STEP
            for axis in range(3):
                before = v_ref[axis, layer] if opening else velocity_ref[axis, layer]
                speed = before + force[axis] * bone_here
                velocity_ref[axis, layer] = speed
                if not last_step:
                    own3[axis, layer] = u_ref[axis, layer] + TIME_STEP * speed

        if not last_step:
            third.pack()
            third.start()

    for part in exchanges:
        part.wait_send()


def body(count_x, count_y, displacement, velocity, bone, broken):
    layers, rows, depth = bone.shape
    bonds = len(every_bond())

    def floats(*shape):
        return pltpu.VMEM(shape, jnp.float32)

    def exchanged(fields):
        packed = packed_rows(fields, layers)
        return [
            floats(fields, layers, rows, depth),
            floats(2, packed, depth),
            floats(2, fields, layers, rows, depth),
            floats(3, 2, packed, depth),
        ]

    words = broken.shape[0]
    packed = packed_rows(words, layers)
    tall = rows + 8
    copies = 4 * len(AROUND) + 5
    scratch = (
        exchanged(4)
        + [
            pltpu.VMEM((2, packed, depth), jnp.int32),
            pltpu.VMEM((1, words, layers, rows, depth), jnp.int32),
            pltpu.VMEM((2, 2, packed, depth), jnp.int32),
        ]
        + exchanged(2)
        + exchanged(3)
        + exchanged(1)
        + [
            floats(2 * REACH + 1, 4, 3 * layers, tall, depth),
            pltpu.VMEM((2 * REACH + 1, words, 2 * layers, tall, depth), jnp.int32),
            floats(2 * REACH + 1, 2, 3 * layers, tall, depth),
            floats(bonds, layers, rows, depth),
            floats(bonds, 3, layers, rows, depth),
            floats(bonds, layers, rows, depth),
            floats(layers, rows, depth),
            pltpu.SemaphoreType.DMA((copies,)),
            pltpu.SemaphoreType.DMA((copies,)),
        ]
    )
    vmem = pl.BlockSpec(memory_space=pltpu.VMEM)
    return pl.pallas_call(
        functools.partial(kernel, count_x, count_y),
        out_shape=(
            jax.ShapeDtypeStruct(velocity.shape, jnp.float32),
            jax.ShapeDtypeStruct(bone.shape, jnp.float32),
        ),
        in_specs=[vmem] * 4,
        out_specs=(vmem, vmem),
        scratch_shapes=scratch,
        compiler_params=pltpu.CompilerParams(collective_id=0, has_side_effects=True),
    )(displacement, velocity, bone, broken)


def solution(mesh):
    in_specs = (
        P(None, "gx", "gy", None),
        P(None, "gx", "gy", None),
        P("gx", "gy", None),
        P(None, "gx", "gy", None),
    )
    out_specs = (P(None, "gx", "gy", None), P("gx", "gy", None))
    run = functools.partial(body, mesh.shape["gx"], mesh.shape["gy"])
    return jax.shard_map(run, mesh=mesh, in_specs=in_specs, out_specs=out_specs, check_vma=False)
```

```python
import functools
import math

import jax
import jax.numpy as jnp
from jax import lax
from jax.experimental import pallas as pl
from jax.experimental.pallas import tpu as pltpu
from jax.sharding import PartitionSpec as P

STEPS = 2
REACH = 3
VMEM_BYTES = 60 * 1024 * 1024

BULK_TERM = -50.0
SHEAR_TERM = 1500.0
TIME_STEP = 0.1
STRETCH_CRITICAL = 0.04
STRETCH_WIDTH = 0.01
DIRECTION_EPS = 1e-06
LOG2_E = math.log2(math.e)

ROW = 4

AROUND = [(dx, dy) for dx in (-1, 0, 1) for dy in (-1, 0, 1) if (dx, dy) != (0, 0)]


def half_bonds():
    listed = []
    for step_x in range(0, 4):
        for step_y in range(-3, 4):
            for step_z in range(-3, 4):
                forward_half = step_x > 0 or (
                    step_x == 0 and (step_y > 0 or (step_y == 0 and step_z > 0))
                )
                if forward_half and step_x * step_x + step_y * step_y + step_z * step_z <= 9:
                    listed.append((step_x, step_y, step_z))
    return listed


def flag_place(number):
    if number < 16:
        return (0, number)
    return (1 + (number - 16) // 15, (number - 16) % 15)


def every_bond():
    listed = []
    for number, (step_x, step_y, step_z) in enumerate(half_bonds()):
        listed.append((step_x, step_y, step_z, number, False))
        listed.append((-step_x, -step_y, -step_z, number, True))
    return listed


def packed_rows(fields, layers):
    return -(-fields * layers * REACH // 8) * 8


class Exchange:
    def __init__(self, own, packed, from_x, from_y, send_sem, recv_sem, base, sides, place, has):
        self.own, self.packed = own, packed
        self.from_x, self.from_y = from_x, from_y
        self.send_sem, self.recv_sem, self.base = send_sem, recv_sem, base
        self.sides, self.place, self.has = sides, place, has
        self.low_dx = min(-dx for dx, dy in sides)

    def copy(self, number):
        dx, dy = self.sides[number]
        if dy == 0:
            source = self.own
            target = self.from_x.at[0 if dx == 1 else 1]
        else:
            source = self.packed.at[0 if dy == -1 else 1]
            target = self.from_y.at[-dx - self.low_dx, 0 if dy == 1 else 1]
        return pltpu.make_async_remote_copy(
            src_ref=source,
            dst_ref=target,
            send_sem=self.send_sem.at[self.base + number],
            recv_sem=self.recv_sem.at[self.base + number],
            device_id={"gx": self.place[0] + dx, "gy": self.place[1] + dy},
            device_id_type=pl.DeviceIdType.MESH,
        )

    def pack(self):
        fields, layers, rows = self.own.shape[:3]
        for field in range(fields):
            for layer in range(layers):
                at = (field * layers + layer) * REACH
                self.packed[0, at : at + REACH] = self.own[field, layer, 0:REACH]
                self.packed[1, at : at + REACH] = self.own[field, layer, rows - REACH : rows]

    def clear(self):
        for dx, dy in self.sides:
            if dy == 0:
                slot = self.from_x.at[0 if dx == 1 else 1]
            else:
                slot = self.from_y.at[-dx - self.low_dx, 0 if dy == 1 else 1]

            @pl.when(jnp.logical_not(self.has(-dx, -dy)))
            def _():
                slot[...] = jnp.zeros(slot.shape, slot.dtype)

    def start(self):
        for number, (dx, dy) in enumerate(self.sides):

            @pl.when(self.has(dx, dy))
            def _():
                self.copy(number).start()

    def wait_recv(self):
        for number, (dx, dy) in enumerate(self.sides):

            @pl.when(self.has(-dx, -dy))
            def _():
                self.copy(number).wait_recv()

    def wait_send(self):
        for number, (dx, dy) in enumerate(self.sides):

            @pl.when(self.has(dx, dy))
            def _():
                self.copy(number).wait_send()

    def assemble(self, extended, dxs):
        fields, layers, rows = self.own.shape[:3]
        for dx in dxs:
            for field in range(fields):
                for layer in range(layers):
                    whole = (dx + 1) * layers + layer
                    at = (field * layers + layer) * REACH
                    if dx == 0:
                        tile = self.own[field, layer]
                    else:
                        tile = self.from_x[0 if dx == -1 else 1, field, layer]
                    y_at = dx - self.low_dx
                    extended[field, whole, ROW : ROW + rows] = tile
                    extended[field, whole, ROW - REACH : ROW] = self.from_y[y_at, 0, at : at + REACH]
                    extended[field, whole, ROW + rows : ROW + rows + REACH] = self.from_y[
                        y_at, 1, at : at + REACH
                    ]


def spread_rolls(rolled, fields, change=None):
    layers, rows, depth = rolled.shape[2:]

    @pl.loop(0, layers)
    def _(layer):
        for field in fields:
            for half in range(0, rows, 8):
                tile = rolled[REACH, field, layer, half : half + 8]
                for step_z in range(-REACH, REACH + 1):
                    if step_z == 0:
                        continue
                    moved = pltpu.roll(tile, (-step_z) % depth, 1)
                    if change is not None:
                        moved = change(moved, field, step_z)
                    rolled[REACH + step_z, field, layer, half : half + 8] = moved


def kernel(
    count_x, count_y,
    u_hbm, v_hbm, bone_hbm, words_hbm,
    velocity_ref, damage_ref,
    u_ref, v_ref, bone_ref, words_ref,
    own1, pack1, fx1, fy1,
    packw, fxw, fyw,
    own2, pack2, fx2, fy2,
    own3, pack3, fx3, fy3,
    own4, pack4, fx4, fy4,
    near, near_words, ratio, masks, pulls, stretches, volumes,
    send_sem, recv_sem, load_sem,
):
    place = (lax.axis_index("gx"), lax.axis_index("gy"))
    layers, rows, depth = bone_ref.shape
    bonds = every_bond()

    def has(dx, dy):
        there = None
        for at, step, count in ((place[0], dx, count_x), (place[1], dy, count_y)):
            if step == 0:
                continue
            good = at > 0 if step < 0 else at < count - 1
            there = good if there is None else jnp.logical_and(there, good)
        return there

    def exchange(own, packed, from_x, from_y, base, sides):
        return Exchange(own, packed, from_x, from_y, send_sem, recv_sem, base, sides, place, has)

    word_sides = [(dx, dy) for dx, dy in AROUND if dx >= 0]
    count = len(AROUND)
    first = exchange(own1, pack1, fx1, fy1, 0, AROUND)
    flags = exchange(words_ref, packw, fxw, fyw, count, word_sides)
    base = count + len(word_sides)
    second = exchange(own2, pack2, fx2, fy2, base, AROUND)
    third = exchange(own3, pack3, fx3, fy3, base + count, AROUND)
    fourth = exchange(own4, pack4, fx4, fy4, base + 2 * count, AROUND)
    exchanges = (first, flags, second, third, fourth)

    loads = [
        pltpu.make_async_copy(source, target, load_sem.at[at])
        for at, (source, target) in enumerate(
            ((u_hbm, u_ref), (bone_hbm, bone_ref), (words_hbm, words_ref), (v_hbm, v_ref))
        )
    ]
    for load in loads:
        load.start()
    barrier = pltpu.get_barrier_semaphore()
    expected = jnp.int32(0)
    for dx, dy in AROUND:
        there = has(dx, dy)
        expected = expected + there.astype(jnp.int32)

        @pl.when(there)
        def _():
            pl.semaphore_signal(
                barrier,
                inc=1,
                device_id={"gx": place[0] + dx, "gy": place[1] + dy},
                device_id_type=pl.DeviceIdType.MESH,
            )

    for part in exchanges:
        part.packed[...] = jnp.zeros(part.packed.shape, part.packed.dtype)
        part.clear()
    for load in loads:
        load.wait()
    for axis in range(3):
        own1[axis] = u_ref[axis]
    own1[3] = bone_ref[...].astype(jnp.float32)
    first.pack()
    flags.pack()
    pl.semaphore_wait(barrier, expected)
    first.start()
    flags.start()

    lane = lax.broadcasted_iota(jnp.int32, (8, depth), 1)

    def shifted(moved, field, step_z):
        if field == 2:
            return moved + float(step_z)
        if field == 3:
            inside = (lane + step_z >= 0) & (lane + step_z < depth)
            return jnp.where(inside, moved, 0.0)
        return moved

    for step_index in range(STEPS):
        opening = step_index == 0
        last_step = step_index == STEPS - 1
        source = first if opening else third
        source.wait_recv()
        source.assemble(near.at[REACH], (-1, 0, 1))
        spread_rolls(near, range(4 if opening else 3), shifted)
        if opening:
            flags.wait_recv()
            flags.assemble(near_words.at[REACH], (-1, 0))
            spread_rolls(near_words, range(4))
        moving = u_ref if opening else own3
        ratios = second if opening else fourth

        @pl.loop(0, layers)
        def _(layer):
            here = [moving[axis, layer] for axis in range(3)]
            total = jnp.zeros((rows, depth), jnp.float32)
            sums = {}
            if opening:
                words_here = [words_ref[word, layer] for word in range(4)]
            for number, (step_x, step_y, step_z, flag, backward) in enumerate(bonds):
                low = ROW + step_y
                rel = []
                for axis, step in enumerate((step_x, step_y, 0)):
                    far = near[REACH + step_z, axis, layer + layers + step_x, low : low + rows]
                    rel.append(far - (here[axis] - float(step)))
                squared = rel[0] * rel[0] + rel[1] * rel[1] + rel[2] * rel[2]
                length = squared * lax.rsqrt(jnp.maximum(squared, 1e-30))
                norm = step_x * step_x + step_y * step_y + step_z * step_z
                natural = math.sqrt(norm)
                extension = length - natural
                power = extension * (LOG2_E / (STRETCH_WIDTH * natural)) - (
                    STRETCH_CRITICAL * LOG2_E / STRETCH_WIDTH
                )
                if opening:
                    word, bit = flag_place(flag)
                    if backward:
                        held = near_words[
                            REACH + step_z, word, layer + layers + step_x, low : low + rows
                        ]
                    else:
                        held = words_here[word]
                    far_bone = near[REACH + step_z, 3, layer + layers + step_x, low : low + rows]
                    intact = jnp.where((held & (1 << bit)) == 0, far_bone, 0.0)
                    masks[number, layer] = intact
                    sums[norm] = sums[norm] + intact if norm in sums else intact
                else:
                    intact = masks[number, layer]
                weight = intact / (1.0 + jnp.exp2(power))
                if last_step:
                    sums[norm] = sums[norm] + weight if norm in sums else weight
                total = total + weight * extension
                stretches[number, layer] = extension * (1.0 / natural)
                pull = weight * lax.rsqrt(squared + DIRECTION_EPS)
                for axis in range(3):
                    pulls[number, axis, layer] = pull * rel[axis]
            bone_here = own1[3, layer]
            weighted = jnp.zeros((rows, depth), jnp.float32)
            for norm, value in sums.items():
                weighted = weighted + value * math.sqrt(norm)
            weighted = weighted * bone_here
            if opening:
                volume = jnp.maximum(weighted, 1.0)
                inverse = 1.0 / volume
                volumes[layer] = inverse
                own2[1, layer] = inverse * SHEAR_TERM
            else:
                inverse = volumes[layer]
            if last_step:
                damage_ref[layer] = 1.0 - weighted * inverse
            scaled = (3.0 * (total * bone_here) * inverse) * inverse
            ratios.own[0, layer] = scaled * BULK_TERM

        ratios.pack()
        ratios.start()
        ratios.wait_recv()
        ratios.assemble(ratio.at[REACH], (-1, 0, 1))
        spread_rolls(ratio, range(2 if opening else 1))

        @pl.loop(0, layers)
        def _(layer):
            scaled = ratios.own[0, layer]
            inverse = own2[1, layer]
            force = [jnp.zeros((rows, depth), jnp.float32) for axis in range(3)]
            for number, (step_x, step_y, step_z, flag, backward) in enumerate(bonds):
                low = ROW + step_y
                far = [
                    ratio[REACH + step_z, kind, layer + layers + step_x, low : low + rows]
                    for kind in range(2)
                ]
                magnitude = (scaled + far[0]) + stretches[number, layer] * (inverse + far[1])
                for axis in range(3):
                    force[axis] = force[axis] + magnitude * pulls[number, axis, layer]
            bone_here = own1[3, layer] * TIME_STEP
            for axis in range(3):
                before = v_ref[axis, layer] if opening else velocity_ref[axis, layer]
                speed = before + force[axis] * bone_here
                velocity_ref[axis, layer] = speed
                if not last_step:
                    own3[axis, layer] = u_ref[axis, layer] + TIME_STEP * speed

        if not last_step:
            third.pack()
            third.start()

    for part in exchanges:
        part.wait_send()


def body(count_x, count_y, displacement, velocity, bone, broken):
    layers, rows, depth = bone.shape
    bonds = len(every_bond())

    def floats(*shape):
        return pltpu.VMEM(shape, jnp.float32)

    def exchanged(fields):
        packed = packed_rows(fields, layers)
        return [
            floats(fields, layers, rows, depth),
            floats(2, packed, depth),
            floats(2, fields, layers, rows, depth),
            floats(3, 2, packed, depth),
        ]

    words = broken.shape[0]
    packed = packed_rows(words, layers)
    tall = rows + 8
    copies = 4 * len(AROUND) + 5
    scratch = (
        [pltpu.VMEM(array.shape, array.dtype) for array in (displacement, velocity, bone, broken)]
        + exchanged(4)
        + [
            pltpu.VMEM((2, packed, depth), jnp.int32),
            pltpu.VMEM((1, words, layers, rows, depth), jnp.int32),
            pltpu.VMEM((2, 2, packed, depth), jnp.int32),
        ]
        + exchanged(2)
        + exchanged(3)
        + exchanged(1)
        + [
            floats(2 * REACH + 1, 4, 3 * layers, tall, depth),
            pltpu.VMEM((2 * REACH + 1, words, 2 * layers, tall, depth), jnp.int32),
            floats(2 * REACH + 1, 2, 3 * layers, tall, depth),
            floats(bonds, layers, rows, depth),
            floats(bonds, 3, layers, rows, depth),
            floats(bonds, layers, rows, depth),
            floats(layers, rows, depth),
            pltpu.SemaphoreType.DMA((copies,)),
            pltpu.SemaphoreType.DMA((copies,)),
            pltpu.SemaphoreType.DMA((4,)),
        ]
    )
    vmem = pl.BlockSpec(memory_space=pltpu.VMEM)
    return pl.pallas_call(
        functools.partial(kernel, count_x, count_y),
        out_shape=(
            jax.ShapeDtypeStruct(velocity.shape, jnp.float32),
            jax.ShapeDtypeStruct(bone.shape, jnp.float32),
        ),
        in_specs=[pl.BlockSpec(memory_space=pltpu.HBM)] * 4,
        out_specs=(vmem, vmem),
        scratch_shapes=scratch,
        compiler_params=pltpu.CompilerParams(
            collective_id=0, has_side_effects=True, vmem_limit_bytes=VMEM_BYTES
        ),
    )(displacement, velocity, bone, broken)


def solution(mesh):
    in_specs = (
        P(None, "gx", "gy", None),
        P(None, "gx", "gy", None),
        P("gx", "gy", None),
        P(None, "gx", "gy", None),
    )
    out_specs = (P(None, "gx", "gy", None), P("gx", "gy", None))
    run = functools.partial(body, mesh.shape["gx"], mesh.shape["gy"])
    return jax.shard_map(run, mesh=mesh, in_specs=in_specs, out_specs=out_specs, check_vma=False)
```

```python
import functools
import math

import jax
import jax.numpy as jnp
from jax import lax
from jax.experimental import pallas as pl
from jax.experimental.pallas import tpu as pltpu
from jax.sharding import PartitionSpec as P

STEPS = 2
REACH = 3
VMEM_BYTES = 60 * 1024 * 1024

BULK_TERM = -50.0
SHEAR_TERM = 1500.0
TIME_STEP = 0.1
STRETCH_CRITICAL = 0.04
STRETCH_WIDTH = 0.01
DIRECTION_EPS = 1e-06
LOG2_E = math.log2(math.e)

ROW = 4

AROUND = [(dx, dy) for dx in (-1, 0, 1) for dy in (-1, 0, 1) if (dx, dy) != (0, 0)]


def half_bonds():
    listed = []
    for step_x in range(0, 4):
        for step_y in range(-3, 4):
            for step_z in range(-3, 4):
                forward_half = step_x > 0 or (
                    step_x == 0 and (step_y > 0 or (step_y == 0 and step_z > 0))
                )
                if forward_half and step_x * step_x + step_y * step_y + step_z * step_z <= 9:
                    listed.append((step_x, step_y, step_z))
    return listed


def flag_place(number):
    if number < 16:
        return (0, number)
    return (1 + (number - 16) // 15, (number - 16) % 15)


def every_bond():
    listed = []
    for number, (step_x, step_y, step_z) in enumerate(half_bonds()):
        listed.append((step_x, step_y, step_z, number, False))
        listed.append((-step_x, -step_y, -step_z, number, True))
    return listed


def packed_rows(fields, layers):
    return -(-fields * layers * REACH // 8) * 8


class Exchange:
    def __init__(self, own, packed, from_x, from_y, send_sem, recv_sem, base, sides, place, has):
        self.own, self.packed = own, packed
        self.from_x, self.from_y = from_x, from_y
        self.send_sem, self.recv_sem, self.base = send_sem, recv_sem, base
        self.sides, self.place, self.has = sides, place, has
        self.low_dx = min(-dx for dx, dy in sides)

    def copy(self, number):
        dx, dy = self.sides[number]
        if dy == 0:
            source = self.own
            target = self.from_x.at[0 if dx == 1 else 1]
        else:
            source = self.packed.at[0 if dy == -1 else 1]
            target = self.from_y.at[-dx - self.low_dx, 0 if dy == 1 else 1]
        return pltpu.make_async_remote_copy(
            src_ref=source,
            dst_ref=target,
            send_sem=self.send_sem.at[self.base + number],
            recv_sem=self.recv_sem.at[self.base + number],
            device_id={"gx": self.place[0] + dx, "gy": self.place[1] + dy},
            device_id_type=pl.DeviceIdType.MESH,
        )

    def pack(self):
        fields, layers, rows = self.own.shape[:3]
        for field in range(fields):
            for layer in range(layers):
                at = (field * layers + layer) * REACH
                self.packed[0, at : at + REACH] = self.own[field, layer, 0:REACH]
                self.packed[1, at : at + REACH] = self.own[field, layer, rows - REACH : rows]

    def clear(self):
        for dx, dy in self.sides:
            if dy == 0:
                slot = self.from_x.at[0 if dx == 1 else 1]
            else:
                slot = self.from_y.at[-dx - self.low_dx, 0 if dy == 1 else 1]

            @pl.when(jnp.logical_not(self.has(-dx, -dy)))
            def _():
                slot[...] = jnp.zeros(slot.shape, slot.dtype)

    def start(self):
        order = sorted(range(len(self.sides)), key=lambda at: (self.sides[at][0] != 0, self.sides[at][1] == 0))
        for number in order:
            dx, dy = self.sides[number]

            @pl.when(self.has(dx, dy))
            def _():
                self.copy(number).start()

    def wait_recv(self, remote):
        for number, (dx, dy) in enumerate(self.sides):
            if (dx != 0) != remote:
                continue

            @pl.when(self.has(-dx, -dy))
            def _():
                self.copy(number).wait_recv()

    def wait_send(self):
        for number, (dx, dy) in enumerate(self.sides):

            @pl.when(self.has(dx, dy))
            def _():
                self.copy(number).wait_send()

    def assemble(self, extended, dxs):
        fields, layers, rows = self.own.shape[:3]
        for dx in dxs:
            for field in range(fields):
                for layer in range(layers):
                    whole = (dx + 1) * layers + layer
                    at = (field * layers + layer) * REACH
                    if dx == 0:
                        tile = self.own[field, layer]
                    else:
                        tile = self.from_x[0 if dx == -1 else 1, field, layer]
                    y_at = dx - self.low_dx
                    extended[field, whole, ROW : ROW + rows] = tile
                    extended[field, whole, ROW - REACH : ROW] = self.from_y[y_at, 0, at : at + REACH]
                    extended[field, whole, ROW + rows : ROW + rows + REACH] = self.from_y[
                        y_at, 1, at : at + REACH
                    ]


def spread_rolls(rolled, fields, first, last, change=None):
    rows, depth = rolled.shape[3:]

    @pl.loop(first, last)
    def _(layer):
        for field in fields:
            for half in range(0, rows, 8):
                tile = rolled[REACH, field, layer, half : half + 8]
                for step_z in range(-REACH, REACH + 1):
                    if step_z == 0:
                        continue
                    moved = pltpu.roll(tile, (-step_z) % depth, 1)
                    if change is not None:
                        moved = change(moved, field, step_z)
                    rolled[REACH + step_z, field, layer, half : half + 8] = moved


def kernel(
    count_x, count_y,
    u_hbm, v_hbm, bone_hbm, words_hbm,
    velocity_ref, damage_ref,
    u_ref, v_ref, bone_ref, words_ref,
    own1, pack1, fx1, fy1,
    packw, fxw, fyw,
    own2, pack2, fx2, fy2,
    own3, pack3, fx3, fy3,
    own4, pack4, fx4, fy4,
    near, near_words, ratio, masks, weights, pulls, stretches, volumes, sums_ref, force_ref,
    send_sem, recv_sem, load_sem,
):
    place = (lax.axis_index("gx"), lax.axis_index("gy"))
    layers, rows, depth = bone_ref.shape
    bonds = every_bond()

    def has(dx, dy):
        there = None
        for at, step, count in ((place[0], dx, count_x), (place[1], dy, count_y)):
            if step == 0:
                continue
            good = at > 0 if step < 0 else at < count - 1
            there = good if there is None else jnp.logical_and(there, good)
        return there

    def exchange(own, packed, from_x, from_y, base, sides):
        return Exchange(own, packed, from_x, from_y, send_sem, recv_sem, base, sides, place, has)

    word_sides = [(dx, dy) for dx, dy in AROUND if dx >= 0]
    count = len(AROUND)
    first = exchange(own1, pack1, fx1, fy1, 0, AROUND)
    flags = exchange(words_ref, packw, fxw, fyw, count, word_sides)
    base = count + len(word_sides)
    second = exchange(own2, pack2, fx2, fy2, base, AROUND)
    third = exchange(own3, pack3, fx3, fy3, base + count, AROUND)
    fourth = exchange(own4, pack4, fx4, fy4, base + 2 * count, AROUND)
    exchanges = (first, flags, second, third, fourth)

    loads = [
        pltpu.make_async_copy(source, target, load_sem.at[at])
        for at, (source, target) in enumerate(
            ((u_hbm, u_ref), (bone_hbm, bone_ref), (words_hbm, words_ref), (v_hbm, v_ref))
        )
    ]
    for load in loads:
        load.start()
    barrier = pltpu.get_barrier_semaphore()
    expected = jnp.int32(0)
    for dx, dy in AROUND:
        there = has(dx, dy)
        expected = expected + there.astype(jnp.int32)

        @pl.when(there)
        def _():
            pl.semaphore_signal(
                barrier,
                inc=1,
                device_id={"gx": place[0] + dx, "gy": place[1] + dy},
                device_id_type=pl.DeviceIdType.MESH,
            )

    for part in exchanges:
        part.packed[...] = jnp.zeros(part.packed.shape, part.packed.dtype)
        part.clear()
    for load in loads:
        load.wait()
    for axis in range(3):
        own1[axis] = u_ref[axis]
    own1[3] = bone_ref[...].astype(jnp.float32)
    first.pack()
    flags.pack()
    pl.semaphore_wait(barrier, expected)
    first.start()
    flags.start()

    lane = lax.broadcasted_iota(jnp.int32, (8, depth), 1)

    def shifted(moved, field, step_z):
        if field == 2:
            return moved + float(step_z)
        if field == 3:
            inside = (lane + step_z >= 0) & (lane + step_z < depth)
            return jnp.where(inside, moved, 0.0)
        return moved

    def bonds_of(layer, remote):
        for number, bond in enumerate(bonds):
            if (0 <= layer + bond[0] < layers) != remote:
                yield (number,) + bond

    def relative(moving, layer, here, step_x, step_y, step_z):
        low = ROW + step_y
        rel = []
        for axis, step in enumerate((step_x, step_y, 0)):
            far = near[REACH + step_z, axis, layer + layers + step_x, low : low + rows]
            rel.append(far - (here[axis] - float(step)))
        return rel, rel[0] * rel[0] + rel[1] * rel[1] + rel[2] * rel[2]

    def put_pulls(number, layer, rel, squared, weight):
        pull = weight * lax.rsqrt(squared + DIRECTION_EPS)
        for axis in range(3):
            pulls[number, axis, layer] = pull * rel[axis]

    def strain(moving, opening, last_step, layer, remote):
        here = [moving[axis, layer] for axis in range(3)]
        total = sums_ref[0, layer] if remote else jnp.zeros((rows, depth), jnp.float32)
        sums = {}
        words_here = [words_ref[word, layer] for word in range(4)] if opening else None
        for number, step_x, step_y, step_z, flag, backward in bonds_of(layer, remote):
            low = ROW + step_y
            rel, squared = relative(moving, layer, here, step_x, step_y, step_z)
            length = squared * lax.rsqrt(jnp.maximum(squared, 1e-30))
            norm = step_x * step_x + step_y * step_y + step_z * step_z
            natural = math.sqrt(norm)
            extension = length - natural
            power = extension * (LOG2_E / (STRETCH_WIDTH * natural)) - (
                STRETCH_CRITICAL * LOG2_E / STRETCH_WIDTH
            )
            if opening:
                word, bit = flag_place(flag)
                if backward:
                    held = near_words[
                        REACH + step_z, word, layer + layers + step_x, low : low + rows
                    ]
                else:
                    held = words_here[word]
                far_bone = near[REACH + step_z, 3, layer + layers + step_x, low : low + rows]
                intact = jnp.where((held & (1 << bit)) == 0, far_bone, 0.0)
                masks[number, layer] = intact
                sums[norm] = sums[norm] + intact if norm in sums else intact
            else:
                intact = masks[number, layer]
            weight = intact / (1.0 + jnp.exp2(power))
            if last_step:
                sums[norm] = sums[norm] + weight if norm in sums else weight
            total = total + weight * extension
            stretches[number, layer] = extension * (1.0 / natural)
            if remote:
                weights[number, layer] = weight
            else:
                put_pulls(number, layer, rel, squared, weight)
        sums_ref[0, layer] = total
        weighted = sums_ref[1, layer] if remote else jnp.zeros((rows, depth), jnp.float32)
        for norm, value in sums.items():
            weighted = weighted + value * math.sqrt(norm)
        sums_ref[1, layer] = weighted

    def direct(moving, layer):
        here = [moving[axis, layer] for axis in range(3)]
        for number, step_x, step_y, step_z, flag, backward in bonds_of(layer, True):
            rel, squared = relative(moving, layer, here, step_x, step_y, step_z)
            put_pulls(number, layer, rel, squared, weights[number, layer])

    def push(ratios, layer, remote):
        scaled = ratios.own[0, layer]
        inverse = own2[1, layer]
        if remote:
            force = [force_ref[axis, layer] for axis in range(3)]
        else:
            force = [jnp.zeros((rows, depth), jnp.float32) for axis in range(3)]
        for number, step_x, step_y, step_z, flag, backward in bonds_of(layer, remote):
            low = ROW + step_y
            far = [
                ratio[REACH + step_z, kind, layer + layers + step_x, low : low + rows]
                for kind in range(2)
            ]
            magnitude = (scaled + far[0]) + stretches[number, layer] * (inverse + far[1])
            for axis in range(3):
                force[axis] = force[axis] + magnitude * pulls[number, axis, layer]
        if not remote:
            for axis in range(3):
                force_ref[axis, layer] = force[axis]
        return force

    def sides_of(remote):
        if remote:
            return (-1, 1), ((0, layers), (2 * layers, 3 * layers))
        return (0,), ((layers, 2 * layers),)

    for step_index in range(STEPS):
        opening = step_index == 0
        last_step = step_index == STEPS - 1
        source = first if opening else third
        moving = u_ref if opening else own3
        ratios = second if opening else fourth
        for remote in (False, True):
            dxs, spans = sides_of(remote)
            source.wait_recv(remote)
            source.assemble(near.at[REACH], dxs)
            for low, high in spans:
                spread_rolls(near, range(4 if opening else 3), low, high, shifted)
            if opening:
                flags.wait_recv(remote)
                flags.assemble(near_words.at[REACH], dxs[:1])
                spread_rolls(near_words, range(4), *spans[0])
            for layer in range(layers):
                strain(moving, opening, last_step, layer, remote)

        for layer in range(layers):
            total = sums_ref[0, layer]
            bone_here = own1[3, layer]
            weighted = sums_ref[1, layer] * bone_here
            if opening:
                volume = jnp.maximum(weighted, 1.0)
                inverse = 1.0 / volume
                volumes[layer] = inverse
                own2[1, layer] = inverse * SHEAR_TERM
            else:
                inverse = volumes[layer]
            if last_step:
                damage_ref[layer] = 1.0 - weighted * inverse
            scaled = (3.0 * (total * bone_here) * inverse) * inverse
            ratios.own[0, layer] = scaled * BULK_TERM

        ratios.pack()
        ratios.start()
        for layer in range(layers):
            direct(moving, layer)
        for remote in (False, True):
            dxs, spans = sides_of(remote)
            ratios.wait_recv(remote)
            ratios.assemble(ratio.at[REACH], dxs)
            for low, high in spans:
                spread_rolls(ratio, range(2 if opening else 1), low, high)
            for layer in range(layers):
                force = push(ratios, layer, remote)
                if not remote:
                    continue
                bone_here = own1[3, layer] * TIME_STEP
                for axis in range(3):
                    before = v_ref[axis, layer] if opening else velocity_ref[axis, layer]
                    speed = before + force[axis] * bone_here
                    velocity_ref[axis, layer] = speed
                    if not last_step:
                        own3[axis, layer] = u_ref[axis, layer] + TIME_STEP * speed

        if not last_step:
            third.pack()
            third.start()

    for part in exchanges:
        part.wait_send()


def body(count_x, count_y, displacement, velocity, bone, broken):
    layers, rows, depth = bone.shape
    bonds = len(every_bond())

    def floats(*shape):
        return pltpu.VMEM(shape, jnp.float32)

    def exchanged(fields):
        packed = packed_rows(fields, layers)
        return [
            floats(fields, layers, rows, depth),
            floats(2, packed, depth),
            floats(2, fields, layers, rows, depth),
            floats(3, 2, packed, depth),
        ]

    words = broken.shape[0]
    packed = packed_rows(words, layers)
    tall = rows + 8
    copies = 4 * len(AROUND) + 5
    scratch = (
        [pltpu.VMEM(array.shape, array.dtype) for array in (displacement, velocity, bone, broken)]
        + exchanged(4)
        + [
            pltpu.VMEM((2, packed, depth), jnp.int32),
            pltpu.VMEM((1, words, layers, rows, depth), jnp.int32),
            pltpu.VMEM((2, 2, packed, depth), jnp.int32),
        ]
        + exchanged(2)
        + exchanged(3)
        + exchanged(1)
        + [
            floats(2 * REACH + 1, 4, 3 * layers, tall, depth),
            pltpu.VMEM((2 * REACH + 1, words, 2 * layers, tall, depth), jnp.int32),
            floats(2 * REACH + 1, 2, 3 * layers, tall, depth),
            floats(bonds, layers, rows, depth),
            floats(bonds, layers, rows, depth),
            floats(bonds, 3, layers, rows, depth),
            floats(bonds, layers, rows, depth),
            floats(layers, rows, depth),
            floats(2, layers, rows, depth),
            floats(3, layers, rows, depth),
            pltpu.SemaphoreType.DMA((copies,)),
            pltpu.SemaphoreType.DMA((copies,)),
            pltpu.SemaphoreType.DMA((4,)),
        ]
    )
    vmem = pl.BlockSpec(memory_space=pltpu.VMEM)
    return pl.pallas_call(
        functools.partial(kernel, count_x, count_y),
        out_shape=(
            jax.ShapeDtypeStruct(velocity.shape, jnp.float32),
            jax.ShapeDtypeStruct(bone.shape, jnp.float32),
        ),
        in_specs=[pl.BlockSpec(memory_space=pltpu.HBM)] * 4,
        out_specs=(vmem, vmem),
        scratch_shapes=scratch,
        compiler_params=pltpu.CompilerParams(
            collective_id=0, has_side_effects=True, vmem_limit_bytes=VMEM_BYTES
        ),
    )(displacement, velocity, bone, broken)


def solution(mesh):
    in_specs = (
        P(None, "gx", "gy", None),
        P(None, "gx", "gy", None),
        P("gx", "gy", None),
        P(None, "gx", "gy", None),
    )
    out_specs = (P(None, "gx", "gy", None), P("gx", "gy", None))
    run = functools.partial(body, mesh.shape["gx"], mesh.shape["gy"])
    return jax.shard_map(run, mesh=mesh, in_specs=in_specs, out_specs=out_specs, check_vma=False)
```

```python
import functools
import math

import jax
import jax.numpy as jnp
from jax import lax
from jax.experimental import pallas as pl
from jax.experimental.pallas import tpu as pltpu
from jax.sharding import PartitionSpec as P

STEPS = 2
REACH = 3
VMEM_BYTES = 60 * 1024 * 1024

BULK_TERM = -50.0
SHEAR_TERM = 1500.0
TIME_STEP = 0.1
STRETCH_CRITICAL = 0.04
STRETCH_WIDTH = 0.01
DIRECTION_EPS = 1e-06
LOG2_E = math.log2(math.e)

ROW = 4

AROUND = [(dx, dy) for dx in (-1, 0, 1) for dy in (-1, 0, 1) if (dx, dy) != (0, 0)]


def half_bonds():
    listed = []
    for step_x in range(0, 4):
        for step_y in range(-3, 4):
            for step_z in range(-3, 4):
                forward_half = step_x > 0 or (
                    step_x == 0 and (step_y > 0 or (step_y == 0 and step_z > 0))
                )
                if forward_half and step_x * step_x + step_y * step_y + step_z * step_z <= 9:
                    listed.append((step_x, step_y, step_z))
    return listed


def flag_place(number):
    if number < 16:
        return (0, number)
    return (1 + (number - 16) // 15, (number - 16) % 15)


def every_bond():
    listed = []
    for number, (step_x, step_y, step_z) in enumerate(half_bonds()):
        listed.append((step_x, step_y, step_z, number, False))
        listed.append((-step_x, -step_y, -step_z, number, True))
    return listed


def packed_rows(fields, layers):
    return -(-fields * layers * REACH // 8) * 8


class Exchange:
    def __init__(self, own, packed, from_x, from_y, send_sem, recv_sem, base, sides, place, has):
        self.own, self.packed = own, packed
        self.from_x, self.from_y = from_x, from_y
        self.send_sem, self.recv_sem, self.base = send_sem, recv_sem, base
        self.sides, self.place, self.has = sides, place, has
        self.low_dx = min(-dx for dx, dy in sides)

    def copy(self, number):
        dx, dy = self.sides[number]
        if dy == 0:
            source = self.own
            target = self.from_x.at[0 if dx == 1 else 1]
        else:
            source = self.packed.at[0 if dy == -1 else 1]
            target = self.from_y.at[-dx - self.low_dx, 0 if dy == 1 else 1]
        return pltpu.make_async_remote_copy(
            src_ref=source,
            dst_ref=target,
            send_sem=self.send_sem.at[self.base + number],
            recv_sem=self.recv_sem.at[self.base + number],
            device_id={"gx": self.place[0] + dx, "gy": self.place[1] + dy},
            device_id_type=pl.DeviceIdType.MESH,
        )

    def pack(self):
        fields, layers, rows = self.own.shape[:3]
        for field in range(fields):
            for layer in range(layers):
                at = (field * layers + layer) * REACH
                self.packed[0, at : at + REACH] = self.own[field, layer, 0:REACH]
                self.packed[1, at : at + REACH] = self.own[field, layer, rows - REACH : rows]

    def clear(self):
        for dx, dy in self.sides:
            if dy == 0:
                slot = self.from_x.at[0 if dx == 1 else 1]
            else:
                slot = self.from_y.at[-dx - self.low_dx, 0 if dy == 1 else 1]

            @pl.when(jnp.logical_not(self.has(-dx, -dy)))
            def _():
                slot[...] = jnp.zeros(slot.shape, slot.dtype)

    def start(self):
        order = sorted(range(len(self.sides)), key=lambda at: (self.sides[at][0] != 0, self.sides[at][1] == 0))
        for number in order:
            dx, dy = self.sides[number]

            @pl.when(self.has(dx, dy))
            def _():
                self.copy(number).start()

    def wait_recv(self, remote):
        for number, (dx, dy) in enumerate(self.sides):
            if (dx != 0) != remote:
                continue

            @pl.when(self.has(-dx, -dy))
            def _():
                self.copy(number).wait_recv()

    def wait_send(self):
        for number, (dx, dy) in enumerate(self.sides):

            @pl.when(self.has(dx, dy))
            def _():
                self.copy(number).wait_send()

    def assemble(self, extended, dxs):
        fields, layers, rows = self.own.shape[:3]
        for dx in dxs:
            for field in range(fields):
                for layer in range(layers):
                    whole = (dx + 1) * layers + layer
                    at = (field * layers + layer) * REACH
                    if dx == 0:
                        tile = self.own[field, layer]
                    else:
                        tile = self.from_x[0 if dx == -1 else 1, field, layer]
                    y_at = dx - self.low_dx
                    extended[field, whole, ROW : ROW + rows] = tile
                    extended[field, whole, ROW - REACH : ROW] = self.from_y[y_at, 0, at : at + REACH]
                    extended[field, whole, ROW + rows : ROW + rows + REACH] = self.from_y[
                        y_at, 1, at : at + REACH
                    ]


def spread_rolls(rolled, fields, first, last, reach, change=None):
    rows, depth = rolled.shape[3:]

    @pl.loop(first, last)
    def _(layer):
        for field in fields:
            for half in range(0, rows, 8):
                tile = rolled[REACH, field, layer, half : half + 8]
                for step_z in range(-reach, reach + 1):
                    if step_z == 0:
                        continue
                    moved = pltpu.roll(tile, (-step_z) % depth, 1)
                    if change is not None:
                        moved = change(moved, field, step_z)
                    rolled[REACH + step_z, field, layer, half : half + 8] = moved


def kernel(
    count_x, count_y,
    u_hbm, v_hbm, bone_hbm, words_hbm,
    velocity_ref, damage_ref,
    u_ref, v_ref, bone_ref, words_ref,
    own1, pack1, fx1, fy1,
    packw, fxw, fyw,
    own2, pack2, fx2, fy2,
    own3, pack3, fx3, fy3,
    own4, pack4, fx4, fy4,
    near, near_words, ratio, masks, weights, pulls, stretches, volumes, sums_ref, force_ref,
    send_sem, recv_sem, load_sem,
):
    place = (lax.axis_index("gx"), lax.axis_index("gy"))
    layers, rows, depth = bone_ref.shape
    bonds = every_bond()

    def has(dx, dy):
        there = None
        for at, step, count in ((place[0], dx, count_x), (place[1], dy, count_y)):
            if step == 0:
                continue
            good = at > 0 if step < 0 else at < count - 1
            there = good if there is None else jnp.logical_and(there, good)
        return there

    def exchange(own, packed, from_x, from_y, base, sides):
        return Exchange(own, packed, from_x, from_y, send_sem, recv_sem, base, sides, place, has)

    word_sides = [(dx, dy) for dx, dy in AROUND if dx >= 0]
    count = len(AROUND)
    first = exchange(own1, pack1, fx1, fy1, 0, AROUND)
    flags = exchange(words_ref, packw, fxw, fyw, count, word_sides)
    base = count + len(word_sides)
    second = exchange(own2, pack2, fx2, fy2, base, AROUND)
    third = exchange(own3, pack3, fx3, fy3, base + count, AROUND)
    fourth = exchange(own4, pack4, fx4, fy4, base + 2 * count, AROUND)
    exchanges = (first, flags, second, third, fourth)

    loads = [
        pltpu.make_async_copy(source, target, load_sem.at[at])
        for at, (source, target) in enumerate(
            ((u_hbm, u_ref), (bone_hbm, bone_ref), (words_hbm, words_ref), (v_hbm, v_ref))
        )
    ]
    for load in loads:
        load.start()
    barrier = pltpu.get_barrier_semaphore()
    expected = jnp.int32(0)
    for dx, dy in AROUND:
        there = has(dx, dy)
        expected = expected + there.astype(jnp.int32)

        @pl.when(there)
        def _():
            pl.semaphore_signal(
                barrier,
                inc=1,
                device_id={"gx": place[0] + dx, "gy": place[1] + dy},
                device_id_type=pl.DeviceIdType.MESH,
            )

    for part in exchanges:
        part.packed[...] = jnp.zeros(part.packed.shape, part.packed.dtype)
        part.clear()
    for load in loads:
        load.wait()
    for axis in range(3):
        own1[axis] = u_ref[axis]
    own1[3] = bone_ref[...].astype(jnp.float32)
    first.pack()
    flags.pack()
    pl.semaphore_wait(barrier, expected)
    first.start()
    flags.start()

    lane = lax.broadcasted_iota(jnp.int32, (8, depth), 1)

    def shifted(moved, field, step_z):
        if field == 2:
            return moved + float(step_z)
        if field == 3:
            inside = (lane + step_z >= 0) & (lane + step_z < depth)
            return jnp.where(inside, moved, 0.0)
        return moved

    def bonds_of(layer, remote):
        for number, bond in enumerate(bonds):
            if (0 <= layer + bond[0] < layers) != remote:
                yield (number,) + bond

    def relative(moving, layer, here, step_x, step_y, step_z):
        low = ROW + step_y
        rel = []
        for axis, step in enumerate((step_x, step_y, 0)):
            far = near[REACH + step_z, axis, layer + layers + step_x, low : low + rows]
            rel.append(far - (here[axis] - float(step)))
        return rel, rel[0] * rel[0] + rel[1] * rel[1] + rel[2] * rel[2]

    def put_pulls(number, layer, rel, squared, weight):
        pull = weight * lax.rsqrt(squared + DIRECTION_EPS)
        for axis in range(3):
            pulls[number, axis, layer] = pull * rel[axis]

    def strain(moving, opening, last_step, layer, remote):
        here = [moving[axis, layer] for axis in range(3)]
        total = sums_ref[0, layer] if remote else jnp.zeros((rows, depth), jnp.float32)
        sums = {}
        words_here = [words_ref[word, layer] for word in range(4)] if opening else None
        for number, step_x, step_y, step_z, flag, backward in bonds_of(layer, remote):
            low = ROW + step_y
            rel, squared = relative(moving, layer, here, step_x, step_y, step_z)
            length = squared * lax.rsqrt(jnp.maximum(squared, 1e-30))
            norm = step_x * step_x + step_y * step_y + step_z * step_z
            natural = math.sqrt(norm)
            extension = length - natural
            power = extension * (LOG2_E / (STRETCH_WIDTH * natural)) - (
                STRETCH_CRITICAL * LOG2_E / STRETCH_WIDTH
            )
            if opening:
                word, bit = flag_place(flag)
                if backward:
                    held = near_words[
                        REACH + step_z, word, layer + layers + step_x, low : low + rows
                    ]
                else:
                    held = words_here[word]
                far_bone = near[REACH + step_z, 3, layer + layers + step_x, low : low + rows]
                intact = jnp.where((held & (1 << bit)) == 0, far_bone, 0.0)
                masks[number, layer] = intact
                sums[norm] = sums[norm] + intact if norm in sums else intact
            else:
                intact = masks[number, layer]
            weight = intact / (1.0 + jnp.exp2(power))
            if last_step:
                sums[norm] = sums[norm] + weight if norm in sums else weight
            total = total + weight * extension
            stretches[number, layer] = extension * (1.0 / natural)
            if remote:
                weights[number, layer] = weight
            else:
                put_pulls(number, layer, rel, squared, weight)
        sums_ref[0, layer] = total
        weighted = sums_ref[1, layer] if remote else jnp.zeros((rows, depth), jnp.float32)
        for norm, value in sums.items():
            weighted = weighted + value * math.sqrt(norm)
        sums_ref[1, layer] = weighted

    def direct(moving, layer):
        here = [moving[axis, layer] for axis in range(3)]
        for number, step_x, step_y, step_z, flag, backward in bonds_of(layer, True):
            rel, squared = relative(moving, layer, here, step_x, step_y, step_z)
            put_pulls(number, layer, rel, squared, weights[number, layer])

    def push(ratios, layer, remote):
        scaled = ratios.own[0, layer]
        inverse = own2[1, layer]
        if remote:
            force = [force_ref[axis, layer] for axis in range(3)]
        else:
            force = [jnp.zeros((rows, depth), jnp.float32) for axis in range(3)]
        for number, step_x, step_y, step_z, flag, backward in bonds_of(layer, remote):
            low = ROW + step_y
            far = [
                ratio[REACH + step_z, kind, layer + layers + step_x, low : low + rows]
                for kind in range(2)
            ]
            magnitude = (scaled + far[0]) + stretches[number, layer] * (inverse + far[1])
            for axis in range(3):
                force[axis] = force[axis] + magnitude * pulls[number, axis, layer]
        if not remote:
            for axis in range(3):
                force_ref[axis, layer] = force[axis]
        return force

    def sides_of(remote):
        if remote:
            spans = ((layers - REACH + 1, layers), (2 * layers, 2 * layers + REACH - 1))
            return (-1, 1), spans, REACH - 1
        return (0,), ((layers, 2 * layers),), REACH

    for step_index in range(STEPS):
        opening = step_index == 0
        last_step = step_index == STEPS - 1
        source = first if opening else third
        moving = u_ref if opening else own3
        ratios = second if opening else fourth
        for remote in (False, True):
            dxs, spans, reach = sides_of(remote)
            source.wait_recv(remote)
            source.assemble(near.at[REACH], dxs)
            for low, high in spans:
                spread_rolls(near, range(4 if opening else 3), low, high, reach, shifted)
            if opening:
                flags.wait_recv(remote)
                flags.assemble(near_words.at[REACH], dxs[:1])
                spread_rolls(near_words, range(4), *spans[0], reach)
            for layer in range(layers):
                strain(moving, opening, last_step, layer, remote)

        for layer in range(layers):
            total = sums_ref[0, layer]
            bone_here = own1[3, layer]
            weighted = sums_ref[1, layer] * bone_here
            if opening:
                volume = jnp.maximum(weighted, 1.0)
                inverse = 1.0 / volume
                volumes[layer] = inverse
                own2[1, layer] = inverse * SHEAR_TERM
            else:
                inverse = volumes[layer]
            if last_step:
                damage_ref[layer] = 1.0 - weighted * inverse
            scaled = (3.0 * (total * bone_here) * inverse) * inverse
            ratios.own[0, layer] = scaled * BULK_TERM

        ratios.pack()
        ratios.start()
        for layer in range(layers):
            direct(moving, layer)
        for remote in (False, True):
            dxs, spans, reach = sides_of(remote)
            ratios.wait_recv(remote)
            ratios.assemble(ratio.at[REACH], dxs)
            for low, high in spans:
                spread_rolls(ratio, range(2 if opening else 1), low, high, reach)
            for layer in range(layers):
                force = push(ratios, layer, remote)
                if not remote:
                    continue
                bone_here = own1[3, layer] * TIME_STEP
                for axis in range(3):
                    before = v_ref[axis, layer] if opening else velocity_ref[axis, layer]
                    speed = before + force[axis] * bone_here
                    velocity_ref[axis, layer] = speed
                    if not last_step:
                        own3[axis, layer] = u_ref[axis, layer] + TIME_STEP * speed

        if not last_step:
            third.pack()
            third.start()

    for part in exchanges:
        part.wait_send()


def body(count_x, count_y, displacement, velocity, bone, broken):
    layers, rows, depth = bone.shape
    bonds = len(every_bond())

    def floats(*shape):
        return pltpu.VMEM(shape, jnp.float32)

    def exchanged(fields):
        packed = packed_rows(fields, layers)
        return [
            floats(fields, layers, rows, depth),
            floats(2, packed, depth),
            floats(2, fields, layers, rows, depth),
            floats(3, 2, packed, depth),
        ]

    words = broken.shape[0]
    packed = packed_rows(words, layers)
    tall = rows + 8
    copies = 4 * len(AROUND) + 5
    scratch = (
        [pltpu.VMEM(array.shape, array.dtype) for array in (displacement, velocity, bone, broken)]
        + exchanged(4)
        + [
            pltpu.VMEM((2, packed, depth), jnp.int32),
            pltpu.VMEM((1, words, layers, rows, depth), jnp.int32),
            pltpu.VMEM((2, 2, packed, depth), jnp.int32),
        ]
        + exchanged(2)
        + exchanged(3)
        + exchanged(1)
        + [
            floats(2 * REACH + 1, 4, 3 * layers, tall, depth),
            pltpu.VMEM((2 * REACH + 1, words, 2 * layers, tall, depth), jnp.int32),
            floats(2 * REACH + 1, 2, 3 * layers, tall, depth),
            floats(bonds, layers, rows, depth),
            floats(bonds, layers, rows, depth),
            floats(bonds, 3, layers, rows, depth),
            floats(bonds, layers, rows, depth),
            floats(layers, rows, depth),
            floats(2, layers, rows, depth),
            floats(3, layers, rows, depth),
            pltpu.SemaphoreType.DMA((copies,)),
            pltpu.SemaphoreType.DMA((copies,)),
            pltpu.SemaphoreType.DMA((4,)),
        ]
    )
    vmem = pl.BlockSpec(memory_space=pltpu.VMEM)
    return pl.pallas_call(
        functools.partial(kernel, count_x, count_y),
        out_shape=(
            jax.ShapeDtypeStruct(velocity.shape, jnp.float32),
            jax.ShapeDtypeStruct(bone.shape, jnp.float32),
        ),
        in_specs=[pl.BlockSpec(memory_space=pltpu.HBM)] * 4,
        out_specs=(vmem, vmem),
        scratch_shapes=scratch,
        compiler_params=pltpu.CompilerParams(
            collective_id=0, has_side_effects=True, vmem_limit_bytes=VMEM_BYTES
        ),
    )(displacement, velocity, bone, broken)


def solution(mesh):
    in_specs = (
        P(None, "gx", "gy", None),
        P(None, "gx", "gy", None),
        P("gx", "gy", None),
        P(None, "gx", "gy", None),
    )
    out_specs = (P(None, "gx", "gy", None), P("gx", "gy", None))
    run = functools.partial(body, mesh.shape["gx"], mesh.shape["gy"])
    return jax.shard_map(run, mesh=mesh, in_specs=in_specs, out_specs=out_specs, check_vma=False)
```
